32 devices in a mesh: box: 8 (over z, y), face: 4 (over x, core).
Axes of the slice: x: 2, y: 2, z: 4, core: 2. Of those that a mesh axis runs over, the one named last changes fastest.
Arguments:
- blocks: bfloat16 [32, 24, 24, 128, 128], P('box', 'face'), may hold values from -1 to 2
- pattern: int32 [32, 24, 24], P('box', 'face'), may hold values from 0 to 1, as said below
- shared: int32 [32, 4], P('box'), may hold values from 0 to 23, as said below
- sketch: bfloat16 [3072, 256], replicated, may hold values from -6 to 6
Outputs:
- merged: bfloat16 [32, 3072, 256], P('box', 'face')
The draws below stay inside these ranges and needn't reach their ends.
Inputs may be any that keep to these rules, and one draw needn't show every extreme that they name: `pattern`: 1 where a block is stored; every diagonal block is stored. `shared`: 4 distinct block indices in increasing order.
All inputs are finite; a program needn't handle non-finite values.
Results may differ from the reference program's by a relative error of at most 0.0085.
Values may be sent and summed in bfloat16 or wider, within the bound.
No kernel may reach another device: no remote copies, remote signals or barrier semaphores. Data moves between devices by JAX's collectives and lax.ppermute only.
A program may use at most 128 MiB of HBM per device.

```python
import math
import jax
import jax.numpy as jnp
from jax import lax

BLK = 128
NB = 24
NI = 4
COLS = 256
ITERS = 4
BOX_DEV = 4
BOXES = 32
ORDER = 3072
N_BOX = 8


def draw_blocks(key, part):
    shape = (BOXES, NB, NB, BLK, BLK)
    sigma = 0.8 / math.sqrt(NI * BLK)
    key_noise = jax.random.fold_in(key, 11)
    key_diag = jax.random.fold_in(key, 12)
    noise = jnp.clip(jax.random.normal(key_noise, shape, jnp.float32), -6.0, 6.0) * sigma
    diag_vals = jnp.exp(jax.random.uniform(key_diag, shape, jnp.float32, math.log(0.6), math.log(1.2)))
    row_block = lax_iota_like(NB, 1)
    col_block = lax_iota_like(NB, 2)
    row_cell = lax_iota_like(BLK, 3)
    col_cell = lax_iota_like(BLK, 4)
    on_diag = jnp.logical_and(row_block == col_block, row_cell == col_cell).astype(jnp.float32)
    return (noise + on_diag * diag_vals).astype(jnp.bfloat16)


def lax_iota_like(length, axis_pos):
    dims = [1, 1, 1, 1, 1]
    dims[axis_pos] = length
    return jnp.arange(length, dtype=jnp.int32).reshape(dims)


def draw_pattern(key, part):
    coins = jax.random.randint(jax.random.fold_in(key, 21), (BOXES, NB, NB), 0, 5)
    stored = (coins < 3).astype(jnp.int32)
    eye_blocks = (jnp.arange(NB, dtype=jnp.int32)[:, None] == jnp.arange(NB, dtype=jnp.int32)[None, :]).astype(jnp.int32)
    return jnp.maximum(stored, eye_blocks[None, :, :])


def draw_shared(key, part):
    keys = jax.random.split(jax.random.fold_in(key, 31), BOXES)

    def pick(one_key):
        order = jax.random.permutation(one_key, NB)
        return jnp.sort(order[:NI]).astype(jnp.int32)
    return jax.vmap(pick)(keys)


def bell_draw(own_key, shape, width, limit, kind=jnp.bfloat16):
    values = width * jax.random.normal(own_key, shape, jnp.float32)
    return jnp.clip(values, min=-limit, max=limit).astype(kind)


def setup_inputs(seed: int = 0) -> dict:
    key_of = jax.random.split(jax.random.key(seed), 5)
    blocks = draw_blocks(jax.random.fold_in(key_of[4], 71), 0)
    pattern = draw_pattern(jax.random.fold_in(key_of[4], 71), 0)
    shared = draw_shared(jax.random.fold_in(key_of[4], 71), 0)
    sketch = bell_draw(key_of[3], (ORDER, COLS), 1.0, 6.0)
    return {"blocks": blocks, "pattern": pattern, "shared": shared, "sketch": sketch}


def one_box(box_blocks, box_pattern, box_shared, sketch_blocks):
    block_ids = jnp.arange(NB, dtype=jnp.int32)
    face_index = box_shared.astype(jnp.int32)
    chosen = face_index[:, None] == block_ids[None, :]
    exterior = 1 - jnp.any(chosen, axis=0).astype(jnp.int32)
    keep_ext = (box_pattern * exterior[None, :]).astype(box_blocks.dtype)
    kept_ext = (box_blocks * keep_ext[:, :, None, None]).astype(jnp.float32)
    sketched = jnp.einsum("ijpq,jqc->ipc", kept_ext, sketch_blocks.astype(jnp.float32), precision=lax.Precision.HIGHEST).astype(jnp.bfloat16)
    side_cols = box_blocks[:, face_index] * box_pattern[:, face_index].astype(box_blocks.dtype)[:, :, None, None]
    inner = side_cols[face_index]
    return sketched, side_cols, inner, face_index


def diagonal_of(inner):
    return jnp.diagonal(jnp.diagonal(inner, axis1=0, axis2=1), axis1=0, axis2=1).astype(jnp.float32)


def reference(blocks, pattern, shared, sketch):
    sketch_blocks = sketch.reshape(NB, BLK, COLS)
    pair_count = BOXES // 2

    def merge_pair(pair_index):
        first_box = (pair_index // BOX_DEV) * 2 * BOX_DEV + pair_index % BOX_DEV
        second_box = first_box + BOX_DEV
        outs = []
        parts = []
        for box_id in (first_box, second_box):
            parts.append(one_box(lax.dynamic_index_in_dim(blocks, box_id, 0, keepdims=False),
                                 lax.dynamic_index_in_dim(pattern, box_id, 0, keepdims=False),
                                 lax.dynamic_index_in_dim(shared, box_id, 0, keepdims=False),
                                 sketch_blocks))
        sketched_a, side_a, inner_a, index_a = parts[0]
        sketched_b, side_b, inner_b, index_b = parts[1]
        wide_a = lax.optimization_barrier(sketched_a).astype(jnp.float32)
        wide_b = lax.optimization_barrier(sketched_b).astype(jnp.float32)
        right_side = wide_a[index_a] + wide_b[index_b]
        diag_sum = diagonal_of(inner_a) + diagonal_of(inner_b)
        inner_fa = inner_a.astype(jnp.float32)
        inner_fb = inner_b.astype(jnp.float32)
        potential = right_side / diag_sum[:, :, None]
        for sweep_index in range(ITERS - 1):
            applied = jnp.einsum("klpq,lqc->kpc", inner_fa, potential, precision=lax.Precision.HIGHEST)
            applied = applied + jnp.einsum("klpq,lqc->kpc", inner_fb, potential, precision=lax.Precision.HIGHEST)
            potential = potential + (right_side - applied) / diag_sum[:, :, None]
        rounded = lax.optimization_barrier(potential.astype(jnp.bfloat16)).astype(jnp.float32)
        for wide, side_cols in ((wide_a, side_a), (wide_b, side_b)):
            correction = jnp.einsum("ikpq,kqc->ipc", side_cols.astype(jnp.float32), rounded, precision=lax.Precision.HIGHEST)
            outs.append((wide - correction).astype(jnp.bfloat16).reshape(NB * BLK, COLS))
        return jnp.stack(outs)

    result = lax.map(merge_pair, jnp.arange(pair_count, dtype=jnp.int32))
    result = result.reshape(N_BOX // 2, BOX_DEV, 2, NB * BLK, COLS)
    return jnp.transpose(result, (0, 2, 1, 3, 4)).reshape(BOXES, NB * BLK, COLS)
```

```python
import functools

import jax
import jax.numpy as jnp
from jax import lax
from jax.experimental import pallas as pl
from jax.experimental.pallas import tpu as pltpu
from jax.sharding import PartitionSpec as P

ITERS = 4
MIB = 1024 * 1024
SKETCH_MIB = 24
SMEM = pl.BlockSpec(memory_space=pltpu.SMEM)
VMEM = pl.BlockSpec(memory_space=pltpu.VMEM)
HBM = pl.BlockSpec(memory_space=pltpu.HBM)


def call(kernel, name, out_shape, mib, in_specs, out_specs, flops=0, moved=0, **kwargs):
    return pl.pallas_call(
        kernel,
        name=name,
        out_shape=out_shape,
        in_specs=in_specs,
        out_specs=out_specs,
        compiler_params=pltpu.CompilerParams(vmem_limit_bytes=mib * MIB),
        cost_estimate=pl.CostEstimate(flops=flops, bytes_accessed=moved, transcendentals=0),
        **kwargs,
    )


def views(table, boxes, row_count):
    first = row_count * boxes
    return (
        lambda box, slot: table[first + box, slot],
        lambda box, row, column: table[row * boxes + box, column],
        lambda index: table[first + boxes, index],
    )


def gather_kernel(table, blocks, send, keep, sems):
    boxes, half, blk, width = keep.shape
    row_count = blocks.shape[1]
    slots = 2 * half
    shared, pattern, pos = views(table, boxes, row_count)
    row_start, core = pos(0), pos(1)

    def each(action):
        for order, (where, target) in enumerate(((1 - core, send), (core, keep))):
            for box in range(boxes):
                for part in range(half):
                    slot = where * half + part
                    row = shared(box, slot) - row_start
                    owned = jnp.logical_and(row >= 0, row < row_count)
                    first = ((order * boxes + box) * half + part) * slots
                    action(box, row, owned, first, target, part)

    def copy(box, row, first, target, part, other):
        return pltpu.make_async_copy(
            blocks.at[box, row, shared(box, other)],
            target.at[box, part, :, pl.ds(other * blk, blk)],
            sems.at[first + other],
        )

    def start(box, row, owned, first, target, part):
        @pl.when(owned)
        def _():
            for other in range(slots):
                copy(box, row, first, target, part, other).start()

    def clear(box, row, owned, first, target, part):
        @pl.when(jnp.logical_not(owned))
        def _():
            target[box, part] = jnp.zeros((blk, width), target.dtype)

    def finish(box, row, owned, first, target, part):
        @pl.when(owned)
        def _():
            for other in range(slots):
                copy(box, row, first, target, part, other).wait()

                @pl.when(pattern(box, row, shared(box, other)) == 0)
                def _():
                    target[box, part, :, pl.ds(other * blk, blk)] = jnp.zeros((blk, blk), target.dtype)

    each(start)
    each(clear)
    each(finish)


def merge_kernel(pos, keep, received, *outs):
    boxes = keep.shape[0]
    for distance, out in enumerate(outs):
        pair = lax.rem(lax.bitwise_xor(pos[2], distance), boxes)
        out[...] = keep[pair] + received[pair]


def side_sum_kernel(*refs):
    ins, out = refs[:-1], refs[-1]
    for side in range(2):
        total = ins[side][...]
        for ref in ins[side + 2 :: 2]:
            total = total + ref[...]
        out[side] = total


def sketch_kernel(table, blocks, sketch, sketched, side, send, keep):
    boxes, row_count, all_blocks, blk, _ = blocks.shape
    slots = keep.shape[1]
    half_cols = keep.shape[3]
    shared, pattern, pos = views(table, boxes, row_count)
    row_start, core = pos(0), pos(1)
    mine = pl.ds(pl.multiple_of(core * half_cols, half_cols), half_cols)
    theirs = pl.ds(pl.multiple_of((1 - core) * half_cols, half_cols), half_cols)

    def one_box(box, carry):
        exterior = []
        for column in range(all_blocks):
            outside = shared(box, 0) != column
            for slot in range(1, slots):
                outside = jnp.logical_and(outside, shared(box, slot) != column)
            exterior.append(jnp.where(outside, 1, 0))
        for row in range(row_count):
            parts = []
            for column in range(all_blocks):
                used = pattern(box, row, column) * exterior[column]
                parts.append(blocks[box, row, column] * used.astype(jnp.float32).astype(blocks.dtype))
            left = jnp.concatenate(parts, axis=1)
            product = jnp.dot(left, sketch[...], preferred_element_type=jnp.float32)
            sketched[box, row * blk : (row + 1) * blk] = product.astype(sketched.dtype)
            for slot in range(slots):
                column = shared(box, slot)
                stored = pattern(box, row, column).astype(jnp.float32).astype(blocks.dtype)
                side[box, row * blk : (row + 1) * blk, slot * blk : (slot + 1) * blk] = (
                    blocks[box, row, column] * stored
                )
        for slot in range(slots):
            row = shared(box, slot) - row_start
            owned = jnp.logical_and(row >= 0, row < row_count)

            @pl.when(owned)
            def _():
                rows = pl.ds(pl.multiple_of(row * blk, blk), blk)
                keep[box, slot] = sketched[box, rows, mine]
                send[box, slot] = sketched[box, rows, theirs]

            @pl.when(jnp.logical_not(owned))
            def _():
                keep[box, slot] = jnp.zeros(keep.shape[2:], keep.dtype)
                send[box, slot] = jnp.zeros(send.shape[2:], send.dtype)

        return carry

    lax.fori_loop(0, boxes, one_box, 0)


def solve_kernel(distances, pos, mine, theirs, *refs):
    rhs_refs, out, system = refs[:distances], refs[distances], refs[distances + 1]
    _, half, blk, width = mine.shape
    slots = 2 * half
    core = pos[1]
    for part, where in ((mine, core), (theirs, 1 - core)):
        for side in range(2):
            rows = pl.ds(pl.multiple_of(where * half * blk, half * blk), half * blk)
            system[rows, side * width : (side + 1) * width] = part[side].reshape(half * blk, width)
    right_side = rhs_refs[0][...].astype(jnp.float32)
    for ref in rhs_refs[1:]:
        right_side = right_side + ref[...].astype(jnp.float32)
    cols = right_side.shape[-1]
    right_side = right_side.reshape(slots * blk, cols)
    eye = lax.broadcasted_iota(jnp.int32, (blk, blk), 0) == lax.broadcasted_iota(jnp.int32, (blk, blk), 1)
    diag = []
    for slot in range(slots):
        rows = slice(slot * blk, (slot + 1) * blk)
        both = system[rows, rows].astype(jnp.float32) + system[
            rows, width + slot * blk : width + (slot + 1) * blk
        ].astype(jnp.float32)
        diag.append(jnp.sum(jnp.where(eye, both, 0.0), axis=1, keepdims=True))
    diag_sum = jnp.concatenate(diag, axis=0)
    potential = right_side / diag_sum
    for sweep in range(ITERS - 1):
        high = potential.astype(jnp.bfloat16)
        low = (potential - high.astype(jnp.float32)).astype(jnp.bfloat16)
        both = jnp.concatenate([high, low], axis=1)
        stacked = jnp.concatenate([both, both], axis=0)
        applied = jnp.dot(system[...], stacked, preferred_element_type=jnp.float32)
        applied = applied[:, :cols] + applied[:, cols:]
        potential = potential + (right_side - applied) / diag_sum
    out[...] = potential.astype(out.dtype).reshape(out.shape)


def correct_kernel(distance, pos, sketched, side, mine, theirs, *refs):
    out, result, sem = refs[-3:]
    boxes = sketched.shape[0]
    slots, blk, cols = mine.shape
    core = pos[1]
    box = lax.rem(lax.bitwise_xor(pos[2], distance), boxes)
    own = mine[...].reshape(slots * blk, cols)
    other = theirs[...].reshape(slots * blk, cols)
    parts = [jnp.where(core == 0, own, other), jnp.where(core == 0, other, own)]
    potential = jnp.concatenate(parts, axis=1)
    correction = jnp.dot(side[box], potential, preferred_element_type=jnp.float32)
    result[...] = (sketched[box].astype(jnp.float32) - correction).astype(result.dtype)
    copy = pltpu.make_async_copy(result, out.at[box], sem)
    copy.start()
    copy.wait()


def local(blocks, pattern, shared, sketch):
    boxes, row_count, all_blocks, blk, _ = blocks.shape
    slots = shared.shape[1]
    half = slots // 2
    cols = sketch.shape[1]
    box_size, face_size = lax.axis_size("box"), lax.axis_size("face")
    chips = face_size
    kind = blocks.dtype
    face, box_index = lax.axis_index("face"), lax.axis_index("box")
    pos = jnp.stack(
        [face * row_count, lax.rem(face, 2), (face // 2) * 2 + lax.rem(box_index, 2)]
    ).astype(jnp.int32)
    table = jnp.concatenate(
        [
            jnp.transpose(pattern, (1, 0, 2)).reshape(row_count * boxes, all_blocks),
            jnp.pad(shared, ((0, 0), (0, all_blocks - slots))),
            jnp.pad(pos[None], ((0, 0), (0, all_blocks - 3))),
        ],
        axis=0,
    )

    def other_core(value):
        pairs = [(f, f ^ 1) for f in range(face_size)]
        return lax.ppermute(value, "face", pairs)

    def chip_at(value, distance):
        pairs = []
        for b in range(box_size):
            for f in range(face_size):
                target = (b ^ (distance & 1)) * face_size + (f ^ (2 * (distance >> 1)))
                pairs.append((b * face_size + f, target))
        return lax.ppermute(value, ("box", "face"), pairs)

    def around(values):
        arrived = {d: chip_at(values[d], d) for d in range(len(values) - 1, 0, -1)}
        return [values[0]] + [arrived[d] for d in range(1, len(values))]

    def merged(keep, received, name):
        shape = jax.ShapeDtypeStruct(keep.shape[1:], kind)
        return call(
            merge_kernel, name, [shape] * chips, 6,
            [SMEM, VMEM, VMEM], [VMEM] * chips, moved=4 * keep.size * 2,
        )(pos, keep, received)

    part_shape = jax.ShapeDtypeStruct((boxes, half, blk, slots * blk), kind)
    send, keep = call(
        gather_kernel, "gather", [part_shape] * 2, 4,
        [SMEM, HBM], [VMEM, VMEM], moved=2 * MIB,
        scratch_shapes=[pltpu.SemaphoreType.DMA((boxes * slots * slots,))],
    )(table, pltpu.with_memory_space_constraint(blocks, pltpu.HBM))
    outs = merged(keep, other_core(send), "merge_blocks")
    arrived = around(outs)

    order = row_count * blk
    half_shape = jax.ShapeDtypeStruct((boxes, slots, blk, cols // 2), kind)
    sketched, side, send_y, keep_y = call(
        sketch_kernel, "sketch",
        [
            jax.ShapeDtypeStruct((boxes, order, cols), kind),
            jax.ShapeDtypeStruct((boxes, order, slots * blk), kind),
            half_shape,
            half_shape,
        ],
        SKETCH_MIB,
        [SMEM, VMEM, VMEM], [VMEM] * 4,
        flops=2 * blocks.size * cols,
        moved=2 * blocks.size,
    )(table, blocks, sketch)

    system_shape = jax.ShapeDtypeStruct((2,) + outs[0].shape, kind)
    mine = call(
        side_sum_kernel, "side_sum", system_shape, 4, [VMEM] * chips, VMEM, moved=3 * MIB // 2
    )(*arrived)
    theirs = other_core(mine)

    outs_y = merged(keep_y, other_core(send_y), "merge_sides")
    arrived_y = around(outs_y)

    potential = call(
        functools.partial(solve_kernel, chips), "solve",
        jax.ShapeDtypeStruct((slots, blk, cols // 2), kind), 16,
        [SMEM] + [VMEM] * (2 + chips), VMEM,
        flops=2 * (ITERS - 1) * 2 * (slots * blk) ** 2 * cols, moved=2 * MIB,
        scratch_shapes=[pltpu.VMEM((slots * blk, 2 * slots * blk), kind)],
    )(pos, mine, theirs, *arrived_y)

    back = around([potential] * boxes)
    out_shape = jax.ShapeDtypeStruct((boxes, order, cols), kind)
    result = None
    for distance, mine in enumerate(back):
        result = call(
            functools.partial(correct_kernel, distance), f"correct_{distance}", out_shape, 4,
            [SMEM, VMEM, VMEM, VMEM, VMEM] + ([] if result is None else [HBM]), HBM,
            flops=2 * order * slots * blk * cols, moved=2 * MIB,
            scratch_shapes=[pltpu.VMEM((order, cols), kind), pltpu.SemaphoreType.DMA],
            input_output_aliases={} if result is None else {5: 0},
        )(pos, sketched, side, mine, other_core(mine), *([] if result is None else [result]))
    return result


def solution(mesh):
    return jax.shard_map(
        local,
        mesh=mesh,
        in_specs=(P("box", "face", None, None, None), P("box", "face", None), P("box", None), P()),
        out_specs=P("box", "face", None),
        check_vma=False,
    )
```

```python
import functools

import jax
import jax.numpy as jnp
from jax import lax
from jax.experimental import pallas as pl
from jax.experimental.pallas import tpu as pltpu
from jax.sharding import PartitionSpec as P


ITERS = 4
MIB = 1024 * 1024
SMEM = pl.BlockSpec(memory_space=pltpu.SMEM)
VMEM = pl.BlockSpec(memory_space=pltpu.VMEM)
ANY = pl.BlockSpec(memory_space=pl.ANY)
HBM = pl.BlockSpec(memory_space=pltpu.HBM)


def call(kernel, out_shape, mib, in_specs, out_specs, flops=0, moved=0, **kwargs):
    return pl.pallas_call(
        kernel,
        out_shape=out_shape,
        in_specs=in_specs,
        out_specs=out_specs,
        compiler_params=pltpu.CompilerParams(vmem_limit_bytes=mib * MIB),
        cost_estimate=pl.CostEstimate(flops=flops, bytes_accessed=moved, transcendentals=0),
        **kwargs,
    )


def place():
    face, box = lax.axis_index("face"), lax.axis_index("box")
    return lax.rem(face, 2), lax.bitwise_or(lax.shift_left(lax.div(face, 2), 1), lax.rem(box, 2))


def box_at(distance, boxes):
    return lax.rem(lax.bitwise_xor(place()[1], distance), boxes)


def gather_kernel(shared, pattern_hbm, blocks, send, keep, pattern, sems):
    boxes, half, blk, width = keep.shape
    row_count = blocks.shape[1]
    slots = 2 * half
    row_start = lax.axis_index("face") * row_count
    core = place()[0]
    last = boxes * slots * slots

    def each(action):
        for order, (where, target) in enumerate(((1 - core, send), (core, keep))):
            for box in range(boxes):
                for part in range(half):
                    slot = where * half + part
                    row = shared[box, slot] - row_start
                    owned = jnp.logical_and(row >= 0, row < row_count)
                    first = ((order * boxes + box) * half + part) * slots
                    action(box, row, owned, first, target, part)

    def copy(box, row, first, target, part, other):
        return pltpu.make_async_copy(
            blocks.at[box, row, shared[box, other]],
            target.at[box, part, :, pl.ds(other * blk, blk)],
            sems.at[first + other],
        )

    def start(box, row, owned, first, target, part):
        @pl.when(owned)
        def _():
            for other in range(slots):
                copy(box, row, first, target, part, other).start()

    def clear(box, row, owned, first, target, part):
        @pl.when(jnp.logical_not(owned))
        def _():
            target[box, part] = jnp.zeros((blk, width), target.dtype)

    def finish(box, row, owned, first, target, part):
        @pl.when(owned)
        def _():
            for other in range(slots):
                copy(box, row, first, target, part, other).wait()

                @pl.when(pattern[row, box, shared[box, other]] == 0)
                def _():
                    target[box, part, :, pl.ds(other * blk, blk)] = jnp.zeros((blk, blk), target.dtype)

    to_scalars = pltpu.make_async_copy(pattern_hbm, pattern, sems.at[last])
    to_scalars.start()
    each(start)
    each(clear)
    to_scalars.wait()
    each(finish)


def merge_kernel(keep, received, *outs):
    for distance, out in enumerate(outs):
        pair = box_at(distance, keep.shape[0])
        out[...] = keep[pair] + received[pair]


def side_sum_kernel(*refs):
    ins, out = refs[:-2], refs[-1]
    for side in range(2):
        total = ins[side][...]
        for ref in ins[side + 2 :: 2]:
            total = total + ref[...]
        out[side] = total


def system_kernel(mine, theirs, system, diag_sum):
    _, half, blk, width = mine.shape
    slots = 2 * half
    core = place()[0]
    for part, where in ((mine, core), (theirs, 1 - core)):
        for side in range(2):
            rows = pl.ds(pl.multiple_of(where * half * blk, half * blk), half * blk)
            system[rows, side * width : (side + 1) * width] = part[side].reshape(half * blk, width)
    eye = lax.broadcasted_iota(jnp.int32, (blk, blk), 0) == lax.broadcasted_iota(jnp.int32, (blk, blk), 1)
    for slot in range(slots):
        rows = slice(slot * blk, (slot + 1) * blk)
        both = system[rows, rows].astype(jnp.float32) + system[
            rows, width + slot * blk : width + (slot + 1) * blk
        ].astype(jnp.float32)
        line = jnp.sum(jnp.where(eye, both, 0.0), axis=1, keepdims=True)
        diag_sum[rows, :] = jnp.broadcast_to(line, (blk, diag_sum.shape[1]))


def masked_row(mask, blocks, box, row):
    parts = [
        blocks[box, row, column] * mask[box, row, column : column + 1] for column in range(blocks.shape[2])
    ]
    return jnp.concatenate(parts, axis=1)


def right_kernel(shared, mask, blocks, sketch, send, keep):
    boxes, row_count = blocks.shape[:2]
    slots, half_cols = keep.shape[1], keep.shape[3]
    row_start = lax.axis_index("face") * row_count
    core = place()[0]

    def one(step, carry):
        box, slot = step // slots, lax.rem(step, slots)
        row = shared[box, slot] - row_start
        owned = jnp.logical_and(row >= 0, row < row_count)

        @pl.when(owned)
        def _():
            left = masked_row(mask, blocks, box, row)
            product = jnp.dot(left, sketch[...], preferred_element_type=jnp.float32).astype(keep.dtype)
            low, high = product[:, :half_cols], product[:, half_cols:]
            keep[box, slot] = jnp.where(core == 0, low, high)
            send[box, slot] = jnp.where(core == 0, high, low)

        @pl.when(jnp.logical_not(owned))
        def _():
            keep[box, slot] = jnp.zeros(keep.shape[2:], keep.dtype)
            send[box, slot] = jnp.zeros(send.shape[2:], send.dtype)

        return carry

    lax.fori_loop(0, boxes * slots, one, 0)


def sketch_kernel(distance, mask, blocks, sketch, sketched):
    boxes, row_count, _, blk, _ = blocks.shape
    box = box_at(distance, boxes)
    for row in range(row_count):
        left = masked_row(mask, blocks, box, row)
        product = jnp.dot(left, sketch[...], preferred_element_type=jnp.float32)
        sketched[row * blk : (row + 1) * blk] = product.astype(sketched.dtype)


def side_kernel(shared, pattern, blocks, order_only, *sides):
    del order_only
    boxes, row_count, _, blk, _ = blocks.shape
    for distance, side in enumerate(sides):
        box = box_at(distance, boxes)
        for slot in range(shared.shape[1]):
            column = shared[box, slot]
            for row in range(row_count):
                stored = jnp.where(pattern[row, box, column] != 0, 1.0, 0.0).astype(blocks.dtype)
                side[row * blk : (row + 1) * blk, slot * blk : (slot + 1) * blk] = (
                    blocks[box, row, column] * stored
                )


def solve_kernel(system, diag_sum, *refs):
    rhs_refs, out = refs[:-1], refs[-1]
    right_side = rhs_refs[0][...].astype(jnp.float32)
    for ref in rhs_refs[1:]:
        right_side = right_side + ref[...].astype(jnp.float32)
    slots, blk, cols = right_side.shape
    right_side = right_side.reshape(slots * blk, cols)
    potential = right_side / diag_sum[...]
    for _ in range(ITERS - 1):
        high = potential.astype(jnp.bfloat16)
        low = (potential - high.astype(jnp.float32)).astype(jnp.bfloat16)
        both = jnp.concatenate([high, low], axis=1)
        stacked = jnp.concatenate([both, both], axis=0)
        applied = jnp.dot(system[...], stacked, preferred_element_type=jnp.float32)
        applied = applied[:, :cols] + applied[:, cols:]
        potential = potential + (right_side - applied) / diag_sum[...]
    out[...] = potential.astype(out.dtype).reshape(out.shape)


def correct_kernel(distance, sketched, side, mine, theirs, *refs):
    out, result, sems = refs[-3:]
    boxes = out.shape[0]
    slots, blk, cols = mine.shape
    order = sketched.shape[0]
    pieces = sems.shape[0]
    core = place()[0]
    box = box_at(distance, boxes)
    own = mine[...].reshape(slots * blk, cols)
    other = theirs[...].reshape(slots * blk, cols)
    parts = [jnp.where(core == 0, own, other), jnp.where(core == 0, other, own)]
    potential = jnp.concatenate(parts, axis=1)
    copies = []
    for piece in range(pieces):
        rows = pl.ds(piece * (order // pieces), order // pieces)
        correction = jnp.dot(side[rows], potential, preferred_element_type=jnp.float32)
        result[rows] = (sketched[rows].astype(jnp.float32) - correction).astype(result.dtype)
        copy = pltpu.make_async_copy(result.at[rows], out.at[box, rows], sems.at[piece])
        copy.start()
        copies.append(copy)
    for copy in copies:
        copy.wait()


def local(blocks, pattern, shared, sketch):
    boxes, row_count, all_blocks, blk, _ = blocks.shape
    slots = shared.shape[1]
    half = slots // 2
    cols = sketch.shape[1]
    box_size, face_size = lax.axis_size("box"), lax.axis_size("face")
    chips = face_size
    kind = blocks.dtype
    by_row = jnp.transpose(pattern, (1, 0, 2))
    outside = jnp.all(shared[:, :, None] != lax.iota(jnp.int32, all_blocks)[None, None, :], axis=1)
    mask = jnp.logical_and(pattern != 0, outside[:, None, :]).astype(kind)
    mask = jnp.broadcast_to(mask[..., None], (boxes, row_count, all_blocks, blk))

    def other_core(value):
        pairs = [(f, f ^ 1) for f in range(face_size)]
        return lax.ppermute(value, "face", pairs)

    def chip_at(value, distance):
        pairs = []
        for b in range(box_size):
            for f in range(face_size):
                target = (b ^ (distance & 1)) * face_size + (f ^ (2 * (distance >> 1)))
                pairs.append((b * face_size + f, target))
        return lax.ppermute(value, ("box", "face"), pairs)

    def around(values):
        return [values[0]] + [chip_at(values[d], d) for d in range(1, len(values))]

    def merged(keep, received):
        shape = jax.ShapeDtypeStruct(keep.shape[1:], kind)
        return call(
            merge_kernel, [shape] * chips, 6,
            [VMEM, VMEM], [VMEM] * chips, moved=4 * keep.size * 2,
        )(keep, received)

    part_shape = jax.ShapeDtypeStruct((boxes, half, blk, slots * blk), kind)
    in_place = lambda value: pltpu.with_memory_space_constraint(value, pltpu.HBM)
    send, keep = call(
        gather_kernel, [part_shape] * 2, 4,
        [SMEM, HBM, HBM], [VMEM, VMEM], moved=2 * MIB,
        scratch_shapes=[
            pltpu.SMEM(by_row.shape, jnp.int32),
            pltpu.SemaphoreType.DMA((boxes * slots * slots + 1,)),
        ],
    )(in_place(shared), in_place(by_row), in_place(blocks))
    outs = merged(keep, other_core(send))
    arrived = around(outs)

    order = row_count * blk
    half_shape = jax.ShapeDtypeStruct((boxes, slots, blk, cols // 2), kind)
    send_y, keep_y = call(
        right_kernel, [half_shape] * 2, 6, [SMEM] + [VMEM] * 3, [VMEM] * 2,
        flops=2 * slots * blk * all_blocks * blk * cols, moved=4 * MIB,
    )(shared, mask, blocks, sketch)
    sketches = [
        call(
            functools.partial(sketch_kernel, distance),
            jax.ShapeDtypeStruct((order, cols), kind), 6, [VMEM] * 3, VMEM,
            flops=2 * order * all_blocks * blk * cols, moved=6 * MIB,
        )(mask, blocks, sketch)
        for distance in range(boxes)
    ]
    outs_y = merged(keep_y, other_core(send_y))
    arrived_y = around(outs_y)

    both_shape = jax.ShapeDtypeStruct((2,) + outs[0].shape, kind)
    mine = call(
        side_sum_kernel, both_shape, 4, [VMEM] * chips + [ANY], VMEM, moved=3 * MIB // 2
    )(*arrived, outs_y[0])
    system, diag_sum = call(
        system_kernel,
        [
            jax.ShapeDtypeStruct((slots * blk, 2 * slots * blk), kind),
            jax.ShapeDtypeStruct((slots * blk, cols // 2), jnp.float32),
        ],
        4, [VMEM, VMEM], [VMEM, VMEM], moved=2 * MIB,
    )(mine, other_core(mine))

    sides = call(
        side_kernel, [jax.ShapeDtypeStruct((order, slots * blk), kind)] * boxes, 6,
        [SMEM, SMEM, VMEM, ANY], [VMEM] * boxes, moved=6 * MIB,
    )(shared, by_row, blocks, sketches[-1])

    potential = call(
        solve_kernel,
        jax.ShapeDtypeStruct((slots, blk, cols // 2), kind), 8,
        [VMEM] * (2 + chips), VMEM,
        flops=2 * (ITERS - 1) * 2 * (slots * blk) ** 2 * cols, moved=2 * MIB,
    )(system, diag_sum, *arrived_y)

    back = around([potential] * boxes)
    out_shape = jax.ShapeDtypeStruct((boxes, order, cols), kind)
    results = []
    for distance, mine in enumerate(back):
        if distance == 1 or distance >= 3:
            earlier = 0 if distance == 1 else distance - 2
            mine, results[earlier] = lax.optimization_barrier((mine, results[earlier]))
        result = results[-1] if results else None
        corrected = call(
            functools.partial(correct_kernel, distance), out_shape, 4,
            [VMEM] * 4 + ([] if result is None else [HBM]), HBM,
            flops=2 * order * slots * blk * cols, moved=2 * MIB,
            scratch_shapes=[pltpu.VMEM((order, cols), kind), pltpu.SemaphoreType.DMA((3,))],
            input_output_aliases={} if result is None else {4: 0},
        )(sketches[distance], sides[distance], mine, other_core(mine), *([] if result is None else [result]))
        results.append(corrected)
    return results[-1]


def solution(mesh):
    return jax.shard_map(
        local,
        mesh=mesh,
        in_specs=(P("box", "face", None, None, None), P("box", "face", None), P("box", None), P()),
        out_specs=P("box", "face", None),
        check_vma=False,
    )
```

```python
import functools

import jax
import jax.numpy as jnp
from jax import lax
from jax.experimental import pallas as pl
from jax.experimental.pallas import tpu as pltpu
from jax.sharding import PartitionSpec as P


ITERS = 4
MIB = 1024 * 1024
SMEM = pl.BlockSpec(memory_space=pltpu.SMEM)
VMEM = pl.BlockSpec(memory_space=pltpu.VMEM)
ANY = pl.BlockSpec(memory_space=pl.ANY)
HBM = pl.BlockSpec(memory_space=pltpu.HBM)


def call(kernel, out_shape, mib, in_specs, out_specs, flops=0, moved=0, **kwargs):
    return pl.pallas_call(
        kernel,
        out_shape=out_shape,
        in_specs=in_specs,
        out_specs=out_specs,
        compiler_params=pltpu.CompilerParams(vmem_limit_bytes=mib * MIB),
        cost_estimate=pl.CostEstimate(flops=flops, bytes_accessed=moved, transcendentals=0),
        **kwargs,
    )


def place():
    face, box = lax.axis_index("face"), lax.axis_index("box")
    return lax.rem(face, 2), lax.bitwise_or(lax.shift_left(lax.div(face, 2), 1), lax.rem(box, 2))


def swapped(step):
    return (step & ~3) | ((step & 1) << 1) | ((step >> 1) & 1)


def distance_of(step):
    return jnp.where(place()[0] == 0, step, swapped(step))


def box_at(step, boxes):
    return lax.rem(lax.bitwise_xor(place()[1], distance_of(step)), boxes)


def gather_kernel(groups, shared, pattern_hbm, blocks, *refs):
    outs, (pattern, sems) = refs[:-2], refs[-2:]
    _, half, blk, width = outs[0].shape
    boxes, row_count = blocks.shape[:2]
    slots = 2 * half
    row_start = lax.axis_index("face") * row_count
    core, chip = place()

    def each(action):
        copied = 0
        for order, group in enumerate(groups):
            for where, target in ((1 - core, outs[2 * order]), (core, outs[2 * order + 1])):
                for index, distance in enumerate(group):
                    box = lax.rem(lax.bitwise_xor(chip, distance), boxes)
                    for part in range(half):
                        slot = where * half + part
                        row = shared[box, slot] - row_start
                        owned = jnp.logical_and(row >= 0, row < row_count)
                        action(box, row, owned, target.at[index, part], sems.at[copied])
                        copied += 1

    def start(box, row, owned, target, sem):
        @pl.when(owned)
        def _():
            for other in range(slots):
                pltpu.make_async_copy(
                    blocks.at[box, row, shared[box, other]], target.at[:, pl.ds(other * blk, blk)], sem
                ).start()

    def clear(box, row, owned, target, sem):
        @pl.when(jnp.logical_not(owned))
        def _():
            target[...] = jnp.zeros((blk, width), target.dtype)

    def finish(box, row, owned, target, sem):
        @pl.when(owned)
        def _():
            pltpu.make_async_copy(target, target, sem).wait()
            for other in range(slots):

                @pl.when(pattern[row, box, shared[box, other]] == 0)
                def _():
                    target[:, pl.ds(other * blk, blk)] = jnp.zeros((blk, blk), target.dtype)

    to_scalars = pltpu.make_async_copy(pattern_hbm, pattern, sems.at[boxes * slots])
    to_scalars.start()
    each(start)
    each(clear)
    to_scalars.wait()
    each(finish)


def merge_kernel(steps, index_of, keep, received, *outs):
    for step, out in zip(steps, outs):
        index = index_of(step)
        out[...] = keep[index] + received[index]


def side_sum_kernel(*refs):
    ins, out = refs[:-2], refs[-1]
    first = place()[0] == 0
    totals = [None, None]

    def add(side, value):
        totals[side] = value if totals[side] is None else totals[side] + value

    for step, ref in enumerate(ins):
        other = swapped(step)
        if other == step:
            add(step & 1, ref[...])
        elif step & 1:
            add(1, jnp.where(first, ref[...], ins[other][...]))
            add(0, jnp.where(first, ins[other][...], ref[...]))
    for side, total in enumerate(totals):
        out[side] = total


def system_kernel(mine, theirs, system, rough, diag_sum):
    _, half, blk, width = mine.shape
    slots = 2 * half
    core = place()[0]
    for part, where in ((mine, core), (theirs, 1 - core)):
        for side in range(2):
            rows = pl.ds(pl.multiple_of(where * half * blk, half * blk), half * blk)
            system[rows, side * width : (side + 1) * width] = part[side].reshape(half * blk, width)
        total = part[0].astype(jnp.float32) + part[1].astype(jnp.float32)
        rough[rows, :] = total.reshape(half * blk, width).astype(rough.dtype)
    eye = lax.broadcasted_iota(jnp.int32, (blk, blk), 0) == lax.broadcasted_iota(jnp.int32, (blk, blk), 1)
    for slot in range(slots):
        rows = slice(slot * blk, (slot + 1) * blk)
        both = system[rows, rows].astype(jnp.float32) + system[
            rows, width + slot * blk : width + (slot + 1) * blk
        ].astype(jnp.float32)
        line = jnp.sum(jnp.where(eye, both, 0.0), axis=1, keepdims=True)
        diag_sum[rows, :] = jnp.broadcast_to(line, (blk, diag_sum.shape[1]))
        rough[rows, rows] = jnp.where(eye, 0.0, both).astype(rough.dtype)


def masked_row(mask, blocks, box, row):
    parts = [
        blocks[box, row, column] * mask[box, row, column : column + 1] for column in range(blocks.shape[2])
    ]
    return jnp.concatenate(parts, axis=1)


def right_kernel(shared, mask, blocks, sketch, send, keep):
    boxes, row_count = blocks.shape[:2]
    slots, half_cols = keep.shape[1], keep.shape[3]
    row_start = lax.axis_index("face") * row_count
    core = place()[0]

    def one(step, carry):
        box, slot = step // slots, lax.rem(step, slots)
        row = shared[box, slot] - row_start
        owned = jnp.logical_and(row >= 0, row < row_count)

        @pl.when(owned)
        def _():
            left = masked_row(mask, blocks, box, row)
            product = jnp.dot(left, sketch[...], preferred_element_type=jnp.float32).astype(keep.dtype)
            low, high = product[:, :half_cols], product[:, half_cols:]
            keep[box, slot] = jnp.where(core == 0, low, high)
            send[box, slot] = jnp.where(core == 0, high, low)

        @pl.when(jnp.logical_not(owned))
        def _():
            keep[box, slot] = jnp.zeros(keep.shape[2:], keep.dtype)
            send[box, slot] = jnp.zeros(send.shape[2:], send.dtype)

        return carry

    lax.fori_loop(0, boxes * slots, one, 0)


def sketch_kernel(step, mask, blocks, sketch, *refs):
    sketched = refs[-1]
    boxes, row_count, _, blk, _ = blocks.shape
    box = box_at(step, boxes)
    for row in range(row_count):
        left = masked_row(mask, blocks, box, row)
        product = jnp.dot(left, sketch[...], preferred_element_type=jnp.float32)
        sketched[row * blk : (row + 1) * blk] = product.astype(sketched.dtype)


def side_kernel(shared, pattern, blocks, order_only, *sides):
    del order_only
    boxes, row_count, _, blk, _ = blocks.shape
    for step, side in enumerate(sides):
        box = box_at(step, boxes)
        for slot in range(shared.shape[1]):
            column = shared[box, slot]
            for row in range(row_count):
                stored = jnp.where(pattern[row, box, column] != 0, 1.0, 0.0).astype(blocks.dtype)
                side[row * blk : (row + 1) * blk, slot * blk : (slot + 1) * blk] = (
                    blocks[box, row, column] * stored
                )


def solve_kernel(system, rough, diag_sum, *refs):
    rhs_refs, out = refs[:-1], refs[-1]
    right_side = rhs_refs[0][...].astype(jnp.float32)
    for ref in rhs_refs[1:]:
        right_side = right_side + ref[...].astype(jnp.float32)
    slots, blk, cols = right_side.shape
    right_side = right_side.reshape(slots * blk, cols)
    potential = right_side / diag_sum[...]
    for sweep in range(ITERS - 1):
        high = potential.astype(jnp.bfloat16)
        low = (potential - high.astype(jnp.float32)).astype(jnp.bfloat16)
        both = jnp.concatenate([high, low], axis=1)
        if sweep < ITERS - 2:
            applied = jnp.dot(rough[...], both, preferred_element_type=jnp.float32)
            potential = (right_side - applied[:, :cols] - applied[:, cols:]) / diag_sum[...]
        else:
            stacked = jnp.concatenate([both, both], axis=0)
            applied = jnp.dot(system[...], stacked, preferred_element_type=jnp.float32)
            applied = applied[:, :cols] + applied[:, cols:]
            potential = potential + (right_side - applied) / diag_sum[...]
    out[...] = potential.astype(out.dtype).reshape(out.shape)


def correct_kernel(steps, *refs):
    out, result, sems = refs[-3:]
    boxes = out.shape[0]
    core = place()[0]
    copies = []
    for index, step in enumerate(steps):
        sketched, side, mine, theirs = refs[4 * index : 4 * index + 4]
        slots, blk, cols = mine.shape
        own = mine[...].reshape(slots * blk, cols)
        other = theirs[...].reshape(slots * blk, cols)
        parts = [jnp.where(core == 0, own, other), jnp.where(core == 0, other, own)]
        potential = jnp.concatenate(parts, axis=1)
        correction = jnp.dot(side[...], potential, preferred_element_type=jnp.float32)
        result[index] = (sketched[...].astype(jnp.float32) - correction).astype(result.dtype)
        copy = pltpu.make_async_copy(result.at[index], out.at[box_at(step, boxes)], sems.at[index])
        copy.start()
        copies.append(copy)
    for copy in copies:
        copy.wait()


def local(blocks, pattern, shared, sketch):
    boxes, row_count, all_blocks, blk, _ = blocks.shape
    slots = shared.shape[1]
    half = slots // 2
    cols = sketch.shape[1]
    box_size, face_size = lax.axis_size("box"), lax.axis_size("face")
    chips = face_size
    kind = blocks.dtype
    by_row = jnp.transpose(pattern, (1, 0, 2))
    outside = jnp.all(shared[:, :, None] != lax.iota(jnp.int32, all_blocks)[None, None, :], axis=1)
    mask = jnp.logical_and(pattern != 0, outside[:, None, :]).astype(kind)
    mask = jnp.broadcast_to(mask[..., None], (boxes, row_count, all_blocks, blk))

    def other_core(value):
        pairs = [(f, f ^ 1) for f in range(face_size)]
        return lax.ppermute(value, "face", pairs)

    def chip_at(value, step):
        pairs = []
        for b in range(box_size):
            for f in range(face_size):
                distance = swapped(step) if f & 1 else step
                target = (b ^ (distance & 1)) * face_size + (f ^ (2 * (distance >> 1)))
                pairs.append((b * face_size + f, target))
        return lax.ppermute(value, ("box", "face"), pairs)

    def around(values):
        arrived = {s: chip_at(values[s], s) for s in range(len(values) - 1, 0, -1)}
        return [values[0]] + [arrived[s] for s in range(1, len(values))]

    def merged(keep, received, steps, index_of):
        shape = jax.ShapeDtypeStruct(keep.shape[1:], kind)
        return call(
            functools.partial(merge_kernel, steps, index_of), [shape] * len(steps), 6,
            [VMEM, VMEM], [VMEM] * len(steps), moved=4 * keep.size * 2,
        )(keep, received)

    early, late = [boxes - 1], list(range(boxes - 1))
    part_shapes = [
        jax.ShapeDtypeStruct((len(group), half, blk, slots * blk), kind)
        for group in (early, late)
        for _ in range(2)
    ]
    in_place = lambda value: pltpu.with_memory_space_constraint(value, pltpu.HBM)
    send_early, keep_early, send_late, keep_late = call(
        functools.partial(gather_kernel, (early, late)), part_shapes, 4,
        [SMEM, HBM, HBM], [VMEM] * 4, moved=2 * MIB,
        scratch_shapes=[
            pltpu.SMEM(by_row.shape, jnp.int32),
            pltpu.SemaphoreType.DMA((boxes * slots + 1,)),
        ],
    )(in_place(shared), in_place(by_row), in_place(blocks))
    first_steps = [s for s in range(chips) if s % boxes in early]
    last_steps = [s for s in range(chips) if s % boxes in late]
    outs = dict(
        zip(
            first_steps,
            merged(
                keep_early, other_core(send_early), first_steps,
                lambda s: 0,
            ),
        )
    )
    outs.update(
        zip(
            last_steps,
            merged(
                keep_late, other_core(send_late), last_steps,
                lambda s: lax.rem(distance_of(s), boxes),
            ),
        )
    )
    arrived = around(outs)

    order = row_count * blk
    half_shape = jax.ShapeDtypeStruct((boxes, slots, blk, cols // 2), kind)
    send_y, keep_y = call(
        right_kernel, [half_shape] * 2, 6, [SMEM] + [VMEM] * 3, [VMEM] * 2,
        flops=2 * slots * blk * all_blocks * blk * cols, moved=4 * MIB,
    )(shared, mask, blocks, sketch)

    def sketch_at(step, *after):
        return call(
            functools.partial(sketch_kernel, step),
            jax.ShapeDtypeStruct((order, cols), kind), 6, [VMEM] * 3 + [ANY] * len(after), VMEM,
            flops=2 * order * all_blocks * blk * cols, moved=6 * MIB,
        )(mask, blocks, sketch, *after)

    outs_y = merged(
        keep_y, other_core(send_y), list(range(chips)),
        lambda s: box_at(s, boxes),
    )
    arrived_y = around(outs_y)

    both_shape = jax.ShapeDtypeStruct((2,) + outs[0].shape, kind)
    mine = call(
        side_sum_kernel, both_shape, 4, [VMEM] * chips + [ANY], VMEM, moved=3 * MIB // 2
    )(*arrived, outs_y[0])
    system, rough, diag_sum = call(
        system_kernel,
        [
            jax.ShapeDtypeStruct((slots * blk, 2 * slots * blk), kind),
            jax.ShapeDtypeStruct((slots * blk, slots * blk), kind),
            jax.ShapeDtypeStruct((slots * blk, cols // 2), jnp.float32),
        ],
        6, [VMEM] * 2, [VMEM] * 3, moved=2 * MIB,
    )(mine, other_core(mine))

    sketches = [sketch_at(s) for s in range(boxes - 1)] + [sketch_at(boxes - 1, diag_sum)]
    sides = call(
        side_kernel, [jax.ShapeDtypeStruct((order, slots * blk), kind)] * boxes, 6,
        [SMEM, SMEM, VMEM, ANY], [VMEM] * boxes, moved=6 * MIB,
    )(shared, by_row, blocks, sketches[-1])

    potential = call(
        solve_kernel,
        jax.ShapeDtypeStruct((slots, blk, cols // 2), kind), 8,
        [VMEM] * (3 + chips), VMEM,
        flops=2 * (ITERS - 1) * 2 * (slots * blk) ** 2 * cols, moved=2 * MIB,
    )(system, rough, diag_sum, *arrived_y)

    back = around([potential] * boxes)
    out_shape = jax.ShapeDtypeStruct((boxes, order, cols), kind)
    theirs = [None] * boxes
    result = []

    def correct(*steps):
        inputs = []
        for s in steps:
            inputs += [sketches[s], sides[s], back[s], theirs[swapped(s)]]
        count = len(inputs)
        corrected = call(
            functools.partial(correct_kernel, steps), out_shape, 2 + 2 * len(steps),
            [VMEM] * count + [HBM] * len(result), HBM,
            flops=2 * len(steps) * order * slots * blk * cols, moved=2 * len(steps) * MIB,
            scratch_shapes=[
                pltpu.VMEM((len(steps), order, cols), kind),
                pltpu.SemaphoreType.DMA((len(steps),)),
            ],
            input_output_aliases={count: 0} if result else {},
        )(*inputs, *result)
        result[:] = [corrected]

    def exchange(*steps):
        if result:
            values, result[0] = lax.optimization_barrier(([back[s] for s in steps], result[0]))
        else:
            values = [back[s] for s in steps]
        for s, value in zip(steps, values):
            theirs[s] = other_core(value)

    exchange(0)
    correct(0)
    exchange(boxes - 1)
    theirs[1:-1] = [other_core(back[s]) for s in range(1, boxes - 1)]
    correct(boxes - 1)
    correct(*range(1, boxes - 1))
    return result[0]


def solution(mesh):
    return jax.shard_map(
        local,
        mesh=mesh,
        in_specs=(P("box", "face", None, None, None), P("box", "face", None), P("box", None), P()),
        out_specs=P("box", "face", None),
        check_vma=False,
    )
```

```python
import functools

import jax
import jax.numpy as jnp
from jax import lax
from jax.experimental import pallas as pl
from jax.experimental.pallas import tpu as pltpu
from jax.sharding import PartitionSpec as P


ITERS = 4
MIB = 1024 * 1024
SMEM = pl.BlockSpec(memory_space=pltpu.SMEM)
VMEM = pl.BlockSpec(memory_space=pltpu.VMEM)
ANY = pl.BlockSpec(memory_space=pl.ANY)
HBM = pl.BlockSpec(memory_space=pltpu.HBM)


def call(kernel, out_shape, mib, in_specs, out_specs, flops=0, moved=0, **kwargs):
    return pl.pallas_call(
        kernel,
        out_shape=out_shape,
        in_specs=in_specs,
        out_specs=out_specs,
        compiler_params=pltpu.CompilerParams(vmem_limit_bytes=mib * MIB),
        cost_estimate=pl.CostEstimate(flops=flops, bytes_accessed=moved, transcendentals=0),
        **kwargs,
    )


def place():
    face, box = lax.axis_index("face"), lax.axis_index("box")
    return lax.rem(face, 2), lax.bitwise_or(lax.shift_left(lax.div(face, 2), 1), lax.rem(box, 2))


def box_at(step, boxes):
    return lax.rem(lax.bitwise_xor(place()[1], step), boxes)


def gather_kernel(groups, shared, pattern_hbm, blocks, *refs):
    outs, (pattern, sems) = refs[:-2], refs[-2:]
    _, half, blk, width = outs[0].shape
    boxes, row_count = blocks.shape[:2]
    slots = 2 * half
    row_start = lax.axis_index("face") * row_count
    core = place()[0]

    def each(action):
        copied = 0
        for order, group in enumerate(groups):
            for where, target in ((1 - core, outs[2 * order]), (core, outs[2 * order + 1])):
                for index, step in enumerate(group):
                    box = box_at(step, boxes)
                    for part in range(half):
                        slot = where * half + part
                        row = shared[box, slot] - row_start
                        owned = jnp.logical_and(row >= 0, row < row_count)
                        action(box, row, owned, target.at[index, part], sems.at[copied])
                        copied += 1

    def start(box, row, owned, target, sem):
        @pl.when(owned)
        def _():
            for other in range(slots):
                pltpu.make_async_copy(
                    blocks.at[box, row, shared[box, other]], target.at[:, pl.ds(other * blk, blk)], sem
                ).start()

    def clear(box, row, owned, target, sem):
        @pl.when(jnp.logical_not(owned))
        def _():
            target[...] = jnp.zeros((blk, width), target.dtype)

    def finish(box, row, owned, target, sem):
        @pl.when(owned)
        def _():
            pltpu.make_async_copy(target, target, sem).wait()
            for other in range(slots):

                @pl.when(pattern[row, box, shared[box, other]] == 0)
                def _():
                    target[:, pl.ds(other * blk, blk)] = jnp.zeros((blk, blk), target.dtype)

    to_scalars = pltpu.make_async_copy(pattern_hbm, pattern, sems.at[boxes * slots])
    to_scalars.start()
    each(start)
    each(clear)
    to_scalars.wait()
    each(finish)


def merge_kernel(steps, index_of, keep, received, *outs):
    for step, out in zip(steps, outs):
        index = index_of(step)
        out[...] = keep[index] + received[index]


def side_sum_kernel(*refs):
    ins, out = refs[:-2], refs[-1]
    for side in range(2):
        total = ins[side][...]
        for ref in ins[side + 2 :: 2]:
            total = total + ref[...]
        out[side] = total


def system_kernel(mine, theirs, system, rough, inverse):
    _, half, blk, width = mine.shape
    slots = 2 * half
    core = place()[0]
    for part, where in ((mine, core), (theirs, 1 - core)):
        for side in range(2):
            rows = pl.ds(pl.multiple_of(where * half * blk, half * blk), half * blk)
            system[rows, side * width : (side + 1) * width] = part[side].reshape(half * blk, width)
        total = part[0].astype(jnp.float32) + part[1].astype(jnp.float32)
        rough[rows, :] = total.reshape(half * blk, width).astype(rough.dtype)
    eye = lax.broadcasted_iota(jnp.int32, (blk, blk), 0) == lax.broadcasted_iota(jnp.int32, (blk, blk), 1)
    for slot in range(slots):
        rows = slice(slot * blk, (slot + 1) * blk)
        both = system[rows, rows].astype(jnp.float32) + system[
            rows, width + slot * blk : width + (slot + 1) * blk
        ].astype(jnp.float32)
        line = jnp.sum(jnp.where(eye, both, 0.0), axis=1, keepdims=True)
        inverse[rows, :] = jnp.broadcast_to(1.0 / line, (blk, inverse.shape[1]))
        rough[rows, rows] = jnp.where(eye, 0.0, both).astype(rough.dtype)


def masked_row(mask, blocks, box, row):
    parts = [
        blocks[box, row, column] * mask[box, row, column : column + 1] for column in range(blocks.shape[2])
    ]
    return jnp.concatenate(parts, axis=1)


def right_kernel(shared, mask, blocks, sketch, send, keep):
    boxes, row_count = blocks.shape[:2]
    slots, half_cols = keep.shape[1], keep.shape[3]
    row_start = lax.axis_index("face") * row_count
    core = place()[0]

    def one(step, carry):
        box, slot = step // slots, lax.rem(step, slots)
        row = shared[box, slot] - row_start
        owned = jnp.logical_and(row >= 0, row < row_count)

        @pl.when(owned)
        def _():
            left = masked_row(mask, blocks, box, row)
            product = jnp.dot(left, sketch[...], preferred_element_type=jnp.float32).astype(keep.dtype)
            low, high = product[:, :half_cols], product[:, half_cols:]
            keep[box, slot] = jnp.where(core == 0, low, high)
            send[box, slot] = jnp.where(core == 0, high, low)

        @pl.when(jnp.logical_not(owned))
        def _():
            keep[box, slot] = jnp.zeros(keep.shape[2:], keep.dtype)
            send[box, slot] = jnp.zeros(send.shape[2:], send.dtype)

        return carry

    lax.fori_loop(0, boxes * slots, one, 0)


def sketch_kernel(step, mask, blocks, sketch, *refs):
    sketched = refs[-1]
    boxes, row_count, _, blk, _ = blocks.shape
    box = box_at(step, boxes)
    for row in range(row_count):
        left = masked_row(mask, blocks, box, row)
        product = jnp.dot(left, sketch[...], preferred_element_type=jnp.float32)
        sketched[row * blk : (row + 1) * blk] = product.astype(sketched.dtype)


def side_kernel(shared, pattern, blocks, order_only, *sides):
    del order_only
    boxes, row_count, _, blk, _ = blocks.shape
    for step, side in enumerate(sides):
        box = box_at(step, boxes)
        for slot in range(shared.shape[1]):
            column = shared[box, slot]
            for row in range(row_count):
                stored = jnp.where(pattern[row, box, column] != 0, 1.0, 0.0).astype(blocks.dtype)
                side[row * blk : (row + 1) * blk, slot * blk : (slot + 1) * blk] = (
                    blocks[box, row, column] * stored
                )


def solve_kernel(system, rough, inverse, *refs):
    rhs_refs, out = refs[:-1], refs[-1]
    right_side = rhs_refs[0][...].astype(jnp.float32)
    for ref in rhs_refs[1:]:
        right_side = right_side + ref[...].astype(jnp.float32)
    slots, blk, cols = right_side.shape
    right_side = right_side.reshape(slots * blk, cols)
    potential = right_side * inverse[...]
    for sweep in range(ITERS - 1):
        high = potential.astype(jnp.bfloat16)
        low = (potential - high.astype(jnp.float32)).astype(jnp.bfloat16)
        both = jnp.concatenate([high, low], axis=1)
        if sweep < ITERS - 2:
            applied = jnp.dot(rough[...], both, preferred_element_type=jnp.float32)
            potential = (right_side - applied[:, :cols] - applied[:, cols:]) * inverse[...]
        else:
            stacked = jnp.concatenate([both, both], axis=0)
            applied = jnp.dot(system[...], stacked, preferred_element_type=jnp.float32)
            applied = applied[:, :cols] + applied[:, cols:]
            potential = potential + (right_side - applied) * inverse[...]
    out[...] = potential.astype(out.dtype).reshape(out.shape)


def correct_kernel(steps, *refs):
    out, result, sems = refs[-3:]
    boxes = out.shape[0]
    core = place()[0]
    copies = []
    for index, step in enumerate(steps):
        sketched, side, mine, theirs = refs[4 * index : 4 * index + 4]
        slots, blk, cols = mine.shape
        own = mine[...].reshape(slots * blk, cols)
        other = theirs[...].reshape(slots * blk, cols)
        parts = [jnp.where(core == 0, own, other), jnp.where(core == 0, other, own)]
        potential = jnp.concatenate(parts, axis=1)
        pieces = sems.shape[0] // len(steps)
        piece = sketched.shape[0] // pieces
        for part in range(pieces):
            rows = pl.ds(part * piece, piece)
            correction = jnp.dot(side[rows], potential, preferred_element_type=jnp.float32)
            result[index, rows] = (sketched[rows].astype(jnp.float32) - correction).astype(result.dtype)
            copy = pltpu.make_async_copy(
                result.at[index, rows], out.at[box_at(step, boxes), rows], sems.at[index * pieces + part]
            )
            copy.start()
            copies.append(copy)
    for copy in copies:
        copy.wait()


def local(blocks, pattern, shared, sketch):
    boxes, row_count, all_blocks, blk, _ = blocks.shape
    slots = shared.shape[1]
    half = slots // 2
    cols = sketch.shape[1]
    box_size, face_size = lax.axis_size("box"), lax.axis_size("face")
    chips = face_size
    kind = blocks.dtype
    by_row = jnp.transpose(pattern, (1, 0, 2))
    outside = jnp.all(shared[:, :, None] != lax.iota(jnp.int32, all_blocks)[None, None, :], axis=1)
    mask = jnp.logical_and(pattern != 0, outside[:, None, :]).astype(kind)
    mask = jnp.broadcast_to(mask[..., None], (boxes, row_count, all_blocks, blk))

    def other_core(value):
        pairs = [(f, f ^ 1) for f in range(face_size)]
        return lax.ppermute(value, "face", pairs)

    def chip_at(value, step):
        pairs = []
        for b in range(box_size):
            for f in range(face_size):
                target = (b ^ (step & 1)) * face_size + (f ^ (2 * (step >> 1)))
                pairs.append((b * face_size + f, target))
        return lax.ppermute(value, ("box", "face"), pairs)

    def around(values):
        arrived = {s: chip_at(values[s], s) for s in range(len(values) - 1, 0, -1)}
        return [values[0]] + [arrived[s] for s in range(1, len(values))]

    def merged(keep, received, steps, index_of):
        shape = jax.ShapeDtypeStruct(keep.shape[1:], kind)
        return call(
            functools.partial(merge_kernel, steps, index_of), [shape] * len(steps), 6,
            [VMEM, VMEM], [VMEM] * len(steps), moved=4 * keep.size * 2,
        )(keep, received)

    early, late = [boxes - 1], list(range(boxes - 1))
    part_shapes = [
        jax.ShapeDtypeStruct((len(group), half, blk, slots * blk), kind)
        for group in (early, late)
        for _ in range(2)
    ]
    in_place = lambda value: pltpu.with_memory_space_constraint(value, pltpu.HBM)
    send_early, keep_early, send_late, keep_late = call(
        functools.partial(gather_kernel, (early, late)), part_shapes, 4,
        [SMEM, HBM, HBM], [VMEM] * 4, moved=2 * MIB,
        scratch_shapes=[
            pltpu.SMEM(by_row.shape, jnp.int32),
            pltpu.SemaphoreType.DMA((boxes * slots + 1,)),
        ],
    )(in_place(shared), in_place(by_row), in_place(blocks))
    first_steps = [s for s in range(chips) if s % boxes in early]
    last_steps = [s for s in range(chips) if s % boxes in late]
    outs = dict(
        zip(
            first_steps,
            merged(
                keep_early, other_core(send_early), first_steps,
                lambda s: 0,
            ),
        )
    )
    outs.update(
        zip(
            last_steps,
            merged(
                keep_late, other_core(send_late), last_steps,
                lambda s: late.index(s % boxes),
            ),
        )
    )
    arrived = around(outs)

    order = row_count * blk
    half_shape = jax.ShapeDtypeStruct((boxes, slots, blk, cols // 2), kind)
    send_y, keep_y = call(
        right_kernel, [half_shape] * 2, 6, [SMEM] + [VMEM] * 3, [VMEM] * 2,
        flops=2 * slots * blk * all_blocks * blk * cols, moved=4 * MIB,
    )(shared, mask, blocks, sketch)

    def sketch_at(step, *after):
        return call(
            functools.partial(sketch_kernel, step),
            jax.ShapeDtypeStruct((order, cols), kind), 6, [VMEM] * 3 + [ANY] * len(after), VMEM,
            flops=2 * order * all_blocks * blk * cols, moved=6 * MIB,
        )(mask, blocks, sketch, *after)

    outs_y = merged(
        keep_y, other_core(send_y), list(range(chips)),
        lambda s: box_at(s, boxes),
    )
    arrived_y = around(outs_y)

    both_shape = jax.ShapeDtypeStruct((2,) + outs[0].shape, kind)
    mine = call(side_sum_kernel, both_shape, 4, [VMEM] * chips + [ANY], VMEM, moved=3 * MIB // 2)(*arrived, outs_y[0])
    system, rough, inverse = call(
        system_kernel,
        [
            jax.ShapeDtypeStruct((slots * blk, 2 * slots * blk), kind),
            jax.ShapeDtypeStruct((slots * blk, slots * blk), kind),
            jax.ShapeDtypeStruct((slots * blk, cols // 2), jnp.float32),
        ],
        6, [VMEM] * 2, [VMEM] * 3, moved=2 * MIB,
    )(mine, other_core(mine))

    sketches = [sketch_at(s) for s in range(boxes)]
    sides = call(
        side_kernel, [jax.ShapeDtypeStruct((order, slots * blk), kind)] * boxes, 6,
        [SMEM, SMEM, VMEM, ANY], [VMEM] * boxes, moved=6 * MIB,
    )(shared, by_row, blocks, sketches[-1])

    potential = call(
        solve_kernel,
        jax.ShapeDtypeStruct((slots, blk, cols // 2), kind), 8,
        [VMEM] * (3 + chips), VMEM,
        flops=2 * (ITERS - 1) * 2 * (slots * blk) ** 2 * cols, moved=2 * MIB,
    )(system, rough, inverse, *arrived_y)

    back = around([potential] * boxes)
    out_shape = jax.ShapeDtypeStruct((boxes, order, cols), kind)
    theirs = [None] * boxes
    result = []
    pieces = 3 if row_count % 3 == 0 else 1

    def correct(*steps):
        inputs = []
        for s in steps:
            inputs += [sketches[s], sides[s], back[s], theirs[s]]
        count = len(inputs)
        corrected = call(
            functools.partial(correct_kernel, steps), out_shape, 2 + 2 * len(steps),
            [VMEM] * count + [HBM] * len(result), HBM,
            flops=2 * len(steps) * order * slots * blk * cols, moved=2 * len(steps) * MIB,
            scratch_shapes=[
                pltpu.VMEM((len(steps), order, cols), kind),
                pltpu.SemaphoreType.DMA((pieces * len(steps),)),
            ],
            input_output_aliases={count: 0} if result else {},
        )(*inputs, *result)
        result[:] = [corrected]

    def exchange(*steps):
        if result:
            values, result[0] = lax.optimization_barrier(([back[s] for s in steps], result[0]))
        else:
            values = [back[s] for s in steps]
        for s, value in zip(steps, values):
            theirs[s] = other_core(value)

    exchange(0)
    correct(0)
    exchange(boxes - 1)
    theirs[1:-1] = [other_core(back[s]) for s in range(1, boxes - 1)]
    correct(boxes - 1)
    correct(*range(1, boxes - 1))
    return result[0]


def solution(mesh):
    return jax.shard_map(
        local,
        mesh=mesh,
        in_specs=(P("box", "face", None, None, None), P("box", "face", None), P("box", None), P()),
        out_specs=P("box", "face", None),
        check_vma=False,
    )
```
